32 devices in a mesh: seq: 8 (over y, x, core), ch: 4 (over z).
Axes of the slice: x: 2, y: 2, z: 4, core: 2. Of those that a mesh axis runs over, the one named last changes fastest.
Arguments:
- inputs: bfloat16 [1536, 131072], P('ch', 'seq'), may hold values from -6 to 6
- gating: bfloat16 [1536, 131072], P('ch', 'seq'), may hold values from -6 to 6
- upstream: bfloat16 [1536, 131072], P('ch', 'seq'), may hold values from -6 to 6
- factor_one: bfloat16 [512, 512], replicated, may hold values from -0.25 to 0.25
- factor_two: bfloat16 [256, 256], replicated, may hold values from -0.375 to 0.375
- factor_three: bfloat16 [256, 256], replicated, may hold values from -0.375 to 0.375
- factor_four: bfloat16 [512, 512], replicated, may hold values from -0.25 to 0.25
- kernel_cols: float32 [1536, 512], P('ch'), may hold values from -4 to 4
- kernel_rows: float32 [1536, 256], P('ch'), may hold values from -4 to 4
Outputs:
- input_grad: bfloat16 [1536, 131072], P('ch', 'seq')
- gating_grad: bfloat16 [1536, 131072], P('ch', 'seq')
- one_grad: float32 [512, 512], replicated
- two_grad: float32 [256, 256], replicated
- three_grad: float32 [256, 256], replicated
- four_grad: float32 [512, 512], replicated
- cols_grad: float32 [1536, 512], P('ch')
- rows_grad: float32 [1536, 256], P('ch')
The draws below stay inside these ranges and needn't reach their ends.
All inputs are finite; a program needn't handle non-finite values.
Results may differ from the reference program's by a relative error of at most 0.0076.
Values may be sent and summed in bfloat16 or wider, within the bound.
A program may use at most 384 MiB of HBM per device.

```python
import math
import jax
import jax.numpy as jnp
from jax import lax

P1 = 256
P2 = 512
C = 1536
TOKENS = 131072


def block_levels(key, shape, cuts, low, largest):
    def one(dim, shards_of):
        draws = jax.random.uniform(jax.random.fold_in(jax.random.fold_in(key, 6), dim), (shards_of,), jnp.float32, low / len(cuts), largest / len(cuts))
        return jnp.repeat(jnp.exp(draws), shape[dim] // shards_of).reshape((-1,) + (1,) * (len(shape) - dim - 1))

    factor_of = one(*cuts[0])
    for cut in cuts[1:]:
        factor_of = factor_of * one(*cut)
    return factor_of


def bell_draw(stream_key, extent, scale, most, split=(), dtype=jnp.bfloat16):
    result = scale * jax.random.normal(stream_key, extent, jnp.float32)
    if split:
        result = result * block_levels(stream_key, extent, split, -0.22, 0.18)
    return jnp.clip(result, -most, most).astype(dtype)


def setup_inputs(seed: int = 0) -> dict:
    streams_of = jax.random.split(jax.random.key(seed), 10)
    inputs = bell_draw(streams_of[0], (C, TOKENS), 1.0, 6.0, ((0, 4), (1, 8)))
    gating = bell_draw(streams_of[1], (C, TOKENS), 1.0, 6.0, ((0, 4), (1, 8)))
    upstream = bell_draw(streams_of[2], (C, TOKENS), 1.0, 6.0, ((0, 4), (1, 8)))
    factor_one = bell_draw(streams_of[3], (P2, P2), P2 ** -0.5, 0.25)
    factor_two = bell_draw(streams_of[4], (P1, P1), P1 ** -0.5, 0.375)
    factor_three = bell_draw(streams_of[5], (P1, P1), P1 ** -0.5, 0.375)
    factor_four = bell_draw(streams_of[6], (P2, P2), P2 ** -0.5, 0.25)
    kernel_cols = bell_draw(streams_of[7], (C, P2), 1.0, 4.0, ((0, 4),), jnp.float32)
    kernel_rows = bell_draw(streams_of[8], (C, P1), 1.0, 4.0, ((0, 4),), jnp.float32)
    return dict(inputs=inputs, gating=gating, upstream=upstream, factor_one=factor_one, factor_two=factor_two, factor_three=factor_three, factor_four=factor_four, kernel_cols=kernel_cols, kernel_rows=kernel_rows)


def mult(form, left, right):
    return jnp.einsum(form, left.astype(jnp.float32), right.astype(jnp.float32), precision=lax.Precision.HIGHEST)

def reference(inputs, gating, upstream, factor_one, factor_two, factor_three, factor_four, kernel_cols, kernel_rows):
    width = math.gcd(C, 64)
    groups = C // width

    def one_group(packed):
        shaped, gate_rows, cotangent, kc, kr = packed
        first_prod = mult('cij,jk->cik', shaped, factor_one)
        first_out = (first_prod * kc[:, None, :]).astype(jnp.bfloat16)
        left_prod = mult('ki,cij->ckj', factor_two, first_out)
        left_out = (left_prod * kr[:, :, None]).astype(jnp.bfloat16)
        second = mult('ki,cij->ckj', factor_three, left_out).astype(jnp.bfloat16)
        final_prod = mult('cij,jk->cik', second, factor_four)
        gate_grad = (cotangent.astype(jnp.float32) * final_prod).astype(jnp.bfloat16)
        up_gate = (cotangent.astype(jnp.float32) * gate_rows.astype(jnp.float32)).astype(jnp.bfloat16)
        grad_four = mult('cij,cik->jk', second, up_gate)
        grad_second = mult('cik,jk->cij', up_gate, factor_four).astype(jnp.bfloat16)
        grad_three = mult('ckj,cij->ki', grad_second, left_out)
        grad_left = mult('ki,ckj->cij', factor_three, grad_second)
        rows_part = lax.optimization_barrier(jnp.sum(grad_left * left_prod, axis=2))
        grad_prod = (grad_left * kr[:, :, None]).astype(jnp.bfloat16)
        grad_two = mult('ckj,cij->ki', grad_prod, first_out)
        grad_first = mult('ki,ckj->cij', factor_two, grad_prod).astype(jnp.bfloat16)
        cols_part = lax.optimization_barrier(jnp.sum(grad_first.astype(jnp.float32) * first_prod, axis=1))
        grad_inner = (grad_first.astype(jnp.float32) * kc[:, None, :]).astype(jnp.bfloat16)
        grad_one = mult('cij,cik->jk', shaped, grad_inner)
        input_part = mult('cik,jk->cij', grad_inner, factor_one).astype(jnp.bfloat16)
        return (input_part, gate_grad, grad_one, grad_two, grad_three, grad_four, cols_part, rows_part)
    packed = (inputs.reshape(groups, width, P1, P2), gating.reshape(groups, width, P1, P2), upstream.reshape(groups, width, P1, P2), kernel_cols.reshape(groups, width, P2), kernel_rows.reshape(groups, width, P1))
    results = lax.map(one_group, packed)
    scale_one = 1.0 / math.sqrt(P1 * C)
    scale_two = 1.0 / math.sqrt(P2 * C)
    input_grad = results[0].reshape(C, TOKENS)
    gating_grad = results[1].reshape(C, TOKENS)
    one_grad = lax.optimization_barrier(jnp.sum(results[2], axis=0)) * scale_one
    two_grad = lax.optimization_barrier(jnp.sum(results[3], axis=0)) * scale_two
    three_grad = lax.optimization_barrier(jnp.sum(results[4], axis=0)) * scale_two
    four_grad = lax.optimization_barrier(jnp.sum(results[5], axis=0)) * scale_one
    cols_grad = results[6].reshape(C, P2) / math.sqrt(P1)
    rows_grad = results[7].reshape(C, P1) / math.sqrt(P2)
    return (input_grad, gating_grad, one_grad, two_grad, three_grad, four_grad, cols_grad, rows_grad)
```

```python
import math

import jax
import jax.numpy as jnp
from jax import lax
from jax.experimental import pallas as pl
from jax.experimental.pallas import tpu as pltpu
from jax.sharding import PartitionSpec as P

P1 = 256
P2 = 512
C = 1536
LANES = 128
TALL = 16
FLT = jnp.float32
HALF = jnp.bfloat16


def nn(a, b):
    return lax.dot_general(a, b, (((1,), (0,)), ((), ())), preferred_element_type=FLT)


def nt(a, b):
    return lax.dot_general(a, b, (((1,), (1,)), ((), ())), preferred_element_type=FLT)


def tn(a, b):
    return lax.dot_general(a, b, (((0,), (0,)), ((), ())), preferred_element_type=FLT)


def gather_rows(ref, rows):
    return jnp.concatenate([ref[:, i * P2 : (i + 1) * P2] for i in range(rows)], axis=0)


def to_channels(value, swap, out_ref, rows):
    for v in range(P2 // LANES):
        swap[v] = value[:, v * LANES : (v + 1) * LANES]
    for c in range(TALL):
        for v in range(P2 // LANES):
            out_ref[c, :, v * LANES : (v + 1) * LANES] = swap[
                v, pl.ds(c, rows, stride=TALL), :
            ].astype(HALF)


def to_rows(in_ref, swap, rows):
    for c in range(TALL):
        for v in range(P2 // LANES):
            swap[v, c * rows : (c + 1) * rows, :] = in_ref[
                c, :, v * LANES : (v + 1) * LANES
            ].astype(FLT)
    return jnp.concatenate(
        [
            jnp.concatenate(
                [swap[v, pl.ds(i, TALL, stride=rows), :].astype(HALF) for i in range(rows)], axis=0
            )
            for v in range(P2 // LANES)
        ],
        axis=1,
    )


def gated(up_ref, gate_ref, rows):
    return jnp.concatenate(
        [
            (
                up_ref[:, i * P2 : (i + 1) * P2].astype(FLT)
                * gate_ref[:, i * P2 : (i + 1) * P2].astype(FLT)
            ).astype(HALF)
            for i in range(rows)
        ],
        axis=0,
    )


def grad_second_body(up_ref, gate_ref, four_ref, out_ref, swap):
    rows = out_ref.shape[1]
    to_channels(nt(gated(up_ref, gate_ref, rows), four_ref[...]), swap, out_ref, rows)


def first_body(in_ref, one_ref, cols_ref, out_ref, swap):
    rows = out_ref.shape[1]
    prod = nn(gather_rows(in_ref, rows), one_ref[...])
    scaled = prod.reshape(rows, TALL, P2) * cols_ref[...][None]
    to_channels(scaled.reshape(rows * TALL, P2), swap, out_ref, rows)


def second_body(first_ref, two_ref, three_ref, rows_ref, out_ref):
    parts, several, rows, _ = first_ref.shape
    for c in range(several):
        first = first_ref[:, c].reshape(parts * rows, P2)
        left = (nn(two_ref[...], first) * rows_ref[c]).astype(HALF)
        out_ref[:, c] = nn(three_ref[...], left).astype(HALF).reshape(parts, rows, P2)


def middle_body(
    first_ref,
    grad_ref,
    two_ref,
    two_t_ref,
    three_t_ref,
    rows_ref,
    out_ref,
    rows_out,
    two_out,
    three_out,
):
    parts, several, rows, _ = first_ref.shape

    @pl.when(pl.program_id(0) == 0)
    def _():
        two_out[...] = jnp.zeros_like(two_out)
        three_out[...] = jnp.zeros_like(three_out)

    for c in range(several):
        first = first_ref[:, c].reshape(parts * rows, P2)
        grad_second = grad_ref[:, c].reshape(parts * rows, P2)
        scale = rows_ref[c]
        left_prod = nn(two_ref[...], first)
        left = (left_prod * scale).astype(HALF)
        grad_left = nn(three_t_ref[...], grad_second)
        three_out[...] += nt(grad_second, left)
        rows_out[c] = jnp.sum(grad_left * left_prod, axis=1, keepdims=True)
        grad_prod = (grad_left * scale).astype(HALF)
        two_out[...] += nt(grad_prod, first)
        out_ref[:, c] = nn(two_t_ref[...], grad_prod).astype(HALF).reshape(parts, rows, P2)


def gating_body(second_ref, up_ref, gate_ref, four_ref, out_ref, four_out, swap):
    rows = second_ref.shape[1]

    @pl.when(pl.program_id(0) == 0)
    def _():
        four_out[...] = jnp.zeros_like(four_out)

    second = to_rows(second_ref, swap, rows)
    final = nn(second, four_ref[...])
    for i in range(rows):
        up = up_ref[:, i * P2 : (i + 1) * P2].astype(FLT)
        out_ref[:, i * P2 : (i + 1) * P2] = (up * final[i * TALL : (i + 1) * TALL]).astype(HALF)
    four_out[...] += tn(second, gated(up_ref, gate_ref, rows))


def input_body(grad_ref, in_ref, one_ref, one_t_ref, cols_ref, out_ref, cols_out, one_out, swap):
    rows = grad_ref.shape[1]

    @pl.when(pl.program_id(0) == 0)
    def _():
        one_out[...] = jnp.zeros_like(one_out)

    grad_first = to_rows(grad_ref, swap, rows).astype(FLT).reshape(rows, TALL, P2)
    shaped = gather_rows(in_ref, rows)
    prod = nn(shaped, one_ref[...]).reshape(rows, TALL, P2)
    cols_out[...] = jnp.sum(grad_first * prod, axis=0)
    inner = (grad_first * cols_ref[...][None]).astype(HALF).reshape(rows * TALL, P2)
    one_out[...] += tn(shaped, inner)
    back = nn(inner, one_t_ref[...]).astype(HALF)
    for i in range(rows):
        out_ref[:, i * P2 : (i + 1) * P2] = back[i * TALL : (i + 1) * TALL]


def call(body, name, grid, in_specs, out_specs, out_shape, scratch, flops, moved, args):
    return pl.pallas_call(
        body,
        name=name,
        grid=(grid,),
        in_specs=in_specs,
        out_specs=out_specs,
        out_shape=out_shape,
        scratch_shapes=scratch,
        compiler_params=pltpu.CompilerParams(
            dimension_semantics=("arbitrary",), vmem_limit_bytes=48 * 2**20
        ),
        cost_estimate=pl.CostEstimate(flops=flops, bytes_accessed=moved, transcendentals=0),
    )(*args)


def local(
    inputs,
    gating,
    upstream,
    factor_one,
    factor_two,
    factor_three,
    factor_four,
    kernel_cols,
    kernel_rows,
):
    width, length = inputs.shape
    parts = lax.axis_size("seq")
    rows = length // P2
    several = width // parts
    few = math.gcd(several, 4)
    tall_grid = width // TALL
    wide_grid = several // few
    size = width * length

    flat = pl.BlockSpec((TALL, length), lambda g: (g, 0))
    cube = pl.BlockSpec((TALL, rows, P2), lambda g: (g, 0, 0))
    cols_spec = pl.BlockSpec((TALL, P2), lambda g: (g, 0))
    big = pl.BlockSpec((P2, P2), lambda g: (0, 0))
    small = pl.BlockSpec((P1, P1), lambda g: (0, 0))
    group = pl.BlockSpec((parts, few, rows, P2), lambda g: (0, g, 0, 0))
    rows_spec = pl.BlockSpec((few, P1, 1), lambda g: (g, 0, 0))
    swap = [pltpu.VMEM((P2 // LANES, rows * TALL, LANES), FLT)]
    cube_shape = jax.ShapeDtypeStruct((width, rows, P2), HALF)
    group_shape = jax.ShapeDtypeStruct((parts, several, rows, P2), HALF)
    flat_shape = jax.ShapeDtypeStruct((width, length), HALF)
    big_shape = jax.ShapeDtypeStruct((P2, P2), FLT)
    small_shape = jax.ShapeDtypeStruct((P1, P1), FLT)
    wide = 2 * size * P2
    tall = 2 * size * P1

    def exchange(x):
        return lax.all_to_all(
            x.reshape(parts, several, rows, P2), "seq", split_axis=0, concat_axis=0
        )

    offset = lax.axis_index("seq") * several
    local_rows = lax.dynamic_slice_in_dim(kernel_rows, offset, several, 0)[:, :, None]

    grad_second = call(
        grad_second_body, "grad_second", tall_grid, [flat, flat, big], cube, cube_shape, swap,
        wide, 6 * size, (upstream, gating, factor_four),
    )
    grad_moved = exchange(grad_second)
    first = call(
        first_body, "first", tall_grid, [flat, big, cols_spec], cube, cube_shape, swap,
        wide, 4 * size, (inputs, factor_one, kernel_cols),
    )
    first_moved = exchange(first)
    second = call(
        second_body, "second", wide_grid, [group, small, small, rows_spec], group, group_shape, [],
        2 * tall, 4 * size, (first_moved, factor_two, factor_three, local_rows),
    )
    second_moved = exchange(second).reshape(width, rows, P2)
    grad_first, rows_part, grad_two, grad_three = call(
        middle_body, "middle", wide_grid, [group, group, small, small, small, rows_spec],
        [group, rows_spec, small, small],
        [group_shape, jax.ShapeDtypeStruct((several, P1, 1), FLT), small_shape, small_shape], [],
        5 * tall, 6 * size,
        (first_moved, grad_moved, factor_two, factor_two.T, factor_three.T, local_rows),
    )
    grad_first_moved = exchange(grad_first).reshape(width, rows, P2)
    gating_grad, grad_four = call(
        gating_body, "gating", tall_grid, [cube, flat, flat, big], [flat, big],
        [flat_shape, big_shape], swap,
        2 * wide, 8 * size, (second_moved, upstream, gating, factor_four),
    )
    input_grad, cols_part, grad_one = call(
        input_body, "input", tall_grid, [cube, flat, big, big, cols_spec],
        [flat, cols_spec, big],
        [flat_shape, jax.ShapeDtypeStruct((width, P2), FLT), big_shape], swap,
        3 * wide, 6 * size,
        (grad_first_moved, inputs, factor_one, factor_one.T, kernel_cols),
    )
    rows_whole = lax.dynamic_update_slice_in_dim(
        jnp.zeros((width, P1), FLT), rows_part[:, :, 0], offset, 0
    )
    rows_sum = lax.psum(rows_whole, "seq")
    two_sum, three_sum, four_sum = lax.psum((grad_two, grad_three, grad_four), ("seq", "ch"))
    cols_sum = lax.psum(cols_part, "seq")
    one_sum = lax.psum(grad_one, ("seq", "ch"))
    scale_one = 1.0 / math.sqrt(P1 * C)
    scale_two = 1.0 / math.sqrt(P2 * C)
    return (
        input_grad,
        gating_grad,
        one_sum * scale_one,
        two_sum * scale_two,
        three_sum * scale_two,
        four_sum * scale_one,
        cols_sum / math.sqrt(P1),
        rows_sum / math.sqrt(P2),
    )


def solution(mesh):
    in_specs = (
        P("ch", "seq"),
        P("ch", "seq"),
        P("ch", "seq"),
        P(),
        P(),
        P(),
        P(),
        P("ch", None),
        P("ch", None),
    )
    out_specs = (P("ch", "seq"), P("ch", "seq"), P(), P(), P(), P(), P("ch", None), P("ch", None))
    return jax.shard_map(local, mesh=mesh, in_specs=in_specs, out_specs=out_specs, check_vma=False)
```
